32 devices in a mesh: grp: 2 (over y), gx: 4 (over z), gy: 2 (over x), gz: 2 (over core).
Axes of the slice: x: 2, y: 2, z: 4, core: 2. Of those that a mesh axis runs over, the one named last changes fastest.
Arguments:
- atom_feats: bfloat16 [8, 2, 128, 2304], P(('grp', 'gx'), 'gy'), parts along dimension 0, may hold values from -6 to 6
- atom_pos: float32 [8, 2, 3, 128], P(('grp', 'gx'), 'gy'), parts along dimension 0, may hold values from 0 to 1
- species: int32 [8, 2, 128], P(('grp', 'gx'), 'gy'), parts along dimension 0, may hold values from 0 to 4
- species_gain: float32 [5, 256], replicated, may hold values from 0.5 to 2
- probe_pos: float32 [3, 8192], P(None, ('grp', 'gx', 'gy', 'gz')), parts along dimension 1, may hold values from 0 to 1
- pair_slot: int32 [64, 4], P(('grp', 'gx', 'gy', 'gz')), parts along dimension 0, may hold values from 0 to 8
- pair_count: int32 [64], P(('grp', 'gx', 'gy', 'gz')), parts along dimension 0, may hold values from 1 to 4, as said below
- w_rad: float32 [3, 8, 256], replicated, may hold values from -0.5 to 0.5
- w_one: bfloat16 [256, 256], replicated, may hold values from -0.375 to 0.375
- w_two: float32 [256], replicated, may hold values from -0.375 to 0.375
- target: float32 [8192], P(('grp', 'gx', 'gy', 'gz')), parts along dimension 0, may hold values from -96 to 96
Outputs:
- density: float32 [8192], P(('grp', 'gx', 'gy', 'gz')), parts along dimension 0
- grad_one: float32 [512, 256], P('grp'), parts along dimension 0
- grad_two: float32 [512], P('grp'), parts along dimension 0
The draws below stay inside these ranges and needn't reach their ends.
There are 2 independent parts, one for each index of `grp`. The reference program is written for one: setup_inputs(seed, part) draws one part's arguments, and reference() takes and returns one part's arrays. A program takes and returns all parts, laid end to end along the dimension named above; an argument that names none is the same for every part. Nothing has to cross between parts.
Inputs may be any that keep to these rules, and one draw needn't show every extreme that they name: `pair_count`: each probe block uses between 1 and 4 entries; some block uses all 4.
All inputs are finite; a program needn't handle non-finite values.
Results may differ from the reference program's by a relative error of at most 0.0061.
Values may be sent and summed in bfloat16 or wider, within the bound.
A program may use at most 64 MiB of HBM per device.

```python
import math
import jax
import jax.numpy as jnp
from jax import lax

C = 256
NRAD = 8
NSPEC = 5
A_BLK = 128
PBLK = 128
NPAIR = 4
P_DEV = 256
GRID_X = 4
GRID_Y = 2
PROBES = 4096
PBLOCKS = 32
N_GY = 2
N_GZ = 2


def draw_pair_count(key, part):
    key_counts, key_place = jax.random.split(jax.random.fold_in(key, 11))
    counts = jax.random.randint(key_counts, (PBLOCKS,), 1, NPAIR + 1)
    place = jax.random.randint(key_place, (), 0, PBLOCKS)
    return counts.at[place].set(NPAIR).astype(jnp.int32)


def draw_target(key, part):
    key_scale, key_heavy, key_values = jax.random.split(jax.random.fold_in(key, 23), 3)
    ndevices = PROBES // P_DEV
    scales = jnp.exp(jax.random.uniform(key_scale, (ndevices,), jnp.float32, math.log(0.5), math.log(2.0)))
    heavy = jax.random.randint(key_heavy, (2,), 0, ndevices)
    marked = jnp.any(jnp.arange(ndevices, dtype=jnp.int32)[:, None] == heavy[None, :], axis=1)
    scales = jnp.where(marked, jnp.float32(16.0), scales)
    values = jnp.clip(jax.random.normal(key_values, (ndevices, P_DEV), jnp.float32), -6.0, 6.0)
    return (values * scales[:, None]).reshape(PROBES).astype(jnp.float32)


def plant(array, key, low, largest):
    dims = array.shape
    spot = [jax.random.randint(jax.random.fold_in(key, axis), (), 0, dims[axis]) for axis in range(len(dims))]
    array = array.at[tuple(spot)].set(low)
    longest = dims.index(max(dims))
    spot[longest] = (spot[longest] + 1) % dims[longest]
    return array.at[tuple(spot)].set(largest)


def block_levels(rng, dims, pieces, low, largest):
    level = 1.0
    for axis_at, shards_of in pieces:
        draws = jax.random.uniform(jax.random.fold_in(jax.random.fold_in(rng, 6), axis_at), (shards_of,), jnp.float32, low / len(pieces), largest / len(pieces))
        level = level * jnp.repeat(jnp.exp(draws), dims[axis_at] // shards_of).reshape((-1,) + (1,) * (len(dims) - 1 - axis_at))
    return level


def scatter_about(own_key, shape, width, most, shards=(), kind=jnp.bfloat16):
    level = block_levels(own_key, shape, shards, -0.22, 0.18) if shards else 1.0
    values = jax.random.normal(own_key, shape, jnp.float32) * width * level
    return jnp.minimum(jnp.maximum(values, -most), most).astype(kind)


def setup_inputs(seed: int = 0, part: int = 0) -> dict:
    arg_keys = jax.random.split(jax.random.key(seed), 12)
    own_keys = jax.random.split(jax.random.fold_in(arg_keys[11], part), 12)
    return {
        "atom_feats": scatter_about(own_keys[0], (GRID_X, GRID_Y, A_BLK, 9 * C), 1.0, 6.0, ((0, 4), (1, 2))),
        "atom_pos": jnp.clip(1.0 * jax.random.uniform(own_keys[1], (GRID_X, GRID_Y, 3, A_BLK), jnp.float32) ** block_levels(own_keys[1], (GRID_X, GRID_Y, 3, A_BLK), ((0, 4), (1, 2)), -0.2, 0.2), 0.0, 1.0),
        "species": plant(jax.random.randint(own_keys[2], (GRID_X, GRID_Y, A_BLK), 0, NSPEC), jax.random.fold_in(own_keys[2], 1), 0, NSPEC - 1).astype(jnp.int32),
        "species_gain": jnp.clip(jnp.exp(jax.random.uniform(arg_keys[3], (NSPEC, C), jnp.float32, math.log(0.5), math.log(2.0))), 0.5, 2.0),
        "probe_pos": jnp.clip(1.0 * jax.random.uniform(own_keys[4], (3, PROBES), jnp.float32) ** block_levels(own_keys[4], (3, PROBES), ((1, 16),), -0.2, 0.2), 0.0, 1.0),
        "pair_slot": plant(jax.random.randint(own_keys[5], (PBLOCKS, NPAIR), 0, 9), jax.random.fold_in(own_keys[5], 1), 0, 8).astype(jnp.int32),
        "pair_count": draw_pair_count(jax.random.fold_in(jax.random.fold_in(arg_keys[11], part), 71), part),
        "w_rad": scatter_about(arg_keys[7], (3, NRAD, C), 0.08, 0.5, (), jnp.float32),
        "w_one": scatter_about(arg_keys[8], (C, C), C ** -0.5, 0.375),
        "w_two": scatter_about(arg_keys[9], (C,), C ** -0.5, 0.375, (), jnp.float32),
        "target": draw_target(jax.random.fold_in(jax.random.fold_in(arg_keys[11], part), 71), part),
    }


side_x = 8.0
side_y = 8.0
side_z = 25.0
cutoff = 4.0
sqrt_three = 1.7320508075688772

def pair_term(probes, atoms_xyz, shift_x, shift_y, table, w_rad):
    nrad = w_rad.shape[1]
    dist_x = (atoms_xyz[0][None, :] + shift_x - probes[0][:, None]) * side_x
    dist_y = (atoms_xyz[1][None, :] + shift_y - probes[1][:, None]) * side_y
    dist_z = (atoms_xyz[2][None, :] - probes[2][:, None]) * side_z
    radius2 = dist_x * dist_x + dist_y * dist_y + dist_z * dist_z
    rc2 = cutoff * cutoff
    smooth = jnp.where(radius2 < rc2, (1.0 - radius2 / rc2) ** 2, 0.0)
    radius = jnp.sqrt(radius2)
    centers = cutoff * jnp.arange(nrad, dtype=jnp.float32) / (nrad - 1)
    gamma = 0.5 * (nrad / cutoff) ** 2
    basis = jnp.exp(-gamma * (radius[None] - centers[:, None, None]) ** 2) * smooth[None]
    harmonics = jnp.stack([jnp.ones_like(dist_x), dist_x / cutoff, dist_y / cutoff, dist_z / cutoff, sqrt_three * dist_x * dist_y / rc2, sqrt_three * dist_y * dist_z / rc2, (3.0 * dist_z * dist_z - radius2) / (2.0 * rc2), sqrt_three * dist_x * dist_z / rc2, sqrt_three * (dist_x * dist_x - dist_y * dist_y) / (2.0 * rc2)], axis=1)
    edges = (basis[:, :, None, :] * harmonics[None]).astype(jnp.bfloat16)
    natoms = atoms_xyz.shape[1]
    nprobe = probes.shape[1]
    edges = edges.reshape(nrad * nprobe, 9 * natoms)
    bounds = ((0, 1), (1, 4), (4, 9))
    total = jnp.zeros((nprobe, table.shape[1]), jnp.float32)
    for degree in range(3):
        low, high = bounds[degree]
        part_sum = jnp.dot(edges[:, low * natoms:high * natoms], table[low * natoms:high * natoms], preferred_element_type=jnp.float32).reshape(nrad, nprobe, -1)
        total = total + lax.optimization_barrier(jnp.sum(part_sum * w_rad[degree][:, None, :], axis=0))
    return total

def reference(atom_feats, atom_pos, species, species_gain, probe_pos, pair_slot, pair_count, w_rad, w_one, w_two, target):
    chans = w_one.shape[0]
    nspec = species_gain.shape[0]
    onehot = (species[..., None] == jnp.arange(nspec, dtype=jnp.int32)).astype(jnp.float32)
    gains = jnp.einsum('xyas,sc->xyac', onehot, species_gain, precision=lax.Precision.HIGHEST)
    scaled = (atom_feats.astype(jnp.float32).reshape(GRID_X, GRID_Y, A_BLK, 9, chans) * gains[:, :, :, None, :]).astype(jnp.bfloat16)
    tables = scaled.transpose(0, 1, 3, 2, 4).reshape(GRID_X, GRID_Y, 9 * A_BLK, chans)
    per_dev = P_DEV // PBLK

    def one_block(block):
        device = block // per_dev
        col_x = device // (N_GY * N_GZ)
        col_y = device // N_GZ % N_GY
        probes = lax.dynamic_slice_in_dim(probe_pos, (block * PBLK).astype(jnp.int32), PBLK, 1)

        def step(total, entry):
            slot_id = pair_slot[block, entry]
            move_x = slot_id // 3 - 1
            move_y = slot_id % 3 - 1
            src_x = (col_x + move_x) % GRID_X
            src_y = (col_y + move_y) % GRID_Y
            pair_sum = pair_term(probes, atom_pos[src_x, src_y], move_x.astype(jnp.float32), move_y.astype(jnp.float32), tables[src_x, src_y], w_rad)
            used = entry < pair_count[block]
            return (total + jnp.where(used, pair_sum, 0.0), None)
        total, unused = lax.scan(step, jnp.zeros((PBLK, chans), jnp.float32), jnp.arange(NPAIR, dtype=jnp.int32))
        return total
    message = lax.map(one_block, jnp.arange(PBLOCKS, dtype=jnp.int32)).reshape(PROBES, chans)
    message_bf = message.astype(jnp.bfloat16)
    pre = jnp.dot(message_bf, w_one, preferred_element_type=jnp.float32)
    sigm = jax.nn.sigmoid(pre)
    act = pre * sigm
    density = lax.optimization_barrier(jnp.sum(act * w_two[None, :], axis=1))
    grad_out = (density - target) * jnp.float32(1.0 / math.sqrt(PROBES))
    dpre = (grad_out[:, None] * w_two[None, :] * sigm * (1.0 + pre * (1.0 - sigm))).astype(jnp.bfloat16)
    grad_one = lax.dot_general(message_bf, dpre, (((0,), (0,)), ((), ())), preferred_element_type=jnp.float32)
    grad_two = lax.optimization_barrier(jnp.sum(grad_out[:, None] * act, axis=0))
    return (density, grad_one, grad_two)
```

```python
import functools
import math

import jax
import jax.numpy as jnp
from jax import lax
from jax.experimental import pallas as pl
from jax.experimental.pallas import tpu as pltpu
from jax.sharding import PartitionSpec as P

MESH = pl.DeviceIdType.MESH
PBLK = 128
side_x = 8.0
side_y = 8.0
side_z = 25.0
cutoff = 4.0
sqrt_three = 1.7320508075688772
CHUNKS = ((1, 2), (2, 4), (4, 6), (6, 8), (8, 9), (0, 1))
DEGREE = (1, 1, 2, 2, 2, 0)
Y_FIRST = (3,)
X_ORDER = (0, 1, 2, 4, 5, 3)
FUSED_CHIPS = 8
ROWS = 16


def kernel(
    nx,
    ny,
    feats_in,
    pos_in,
    spec_in,
    gain_in,
    probe_in,
    slot_in,
    count_in,
    w_rad_in,
    w_one_in,
    w_two_in,
    target_in,
    density_out,
    one_out,
    two_out,
    feats,
    pos,
    spec,
    gain,
    probe,
    slot,
    count,
    w_rad,
    w_one,
    w_two,
    target,
    load_sem,
    tab0,
    tab1,
    tab2,
    tab3,
    tab4,
    tab5,
    posb,
    edges,
    pmap,
    msg,
    ici_send,
    ici_recv,
    sib_send,
    sib_recv,
    pos_send,
    pos_recv,
    *reduce_refs,
):
    tabs = (tab0, tab1, tab2, tab3, tab4, tab5)
    nentry = slot.shape[1]
    nblocks = slot.shape[0]
    nrad = w_rad.shape[1]
    natoms, chans = tab0.shape[2], tab0.shape[3]
    dys = (0, 1) if ny == 2 else (0, 1, -1)
    dxs = (0, 1, -1)
    nyc = len(dys)
    ncol = 3 * nyc
    gx, gy, gz = lax.axis_index("gx"), lax.axis_index("gy"), lax.axis_index("gz")
    sibling = {"gz": 1 - gz}

    def at(dx, dy):
        return {"gx": lax.rem(gx + dx + nx, nx), "gy": lax.rem(gy + dy + ny, ny)}

    remote = [(xi, yi) for xi in range(3) for yi in range(nyc) if (xi, yi) != (0, 0)]
    chips = nx * ny
    me = gx * ny + gy
    offsets = range(1, chips)

    def peer(offset):
        other = lax.rem(me + offset, chips)
        return {"gx": other // ny, "gy": lax.rem(other, ny)}

    barrier = pltpu.get_barrier_semaphore()
    if reduce_refs:
        greeted = [peer(offset) for offset in offsets]
    else:
        greeted = [at(-dxs[xi], -dys[yi]) for xi, yi in remote]
    for device in greeted:
        pl.semaphore_signal(barrier, inc=1, device_id=device, device_id_type=MESH)
    pl.semaphore_signal(barrier, inc=1, device_id=sibling, device_id_type=MESH)
    sources = (
        feats_in,
        pos_in,
        spec_in,
        gain_in,
        probe_in,
        slot_in,
        count_in,
        w_rad_in,
        w_one_in,
        w_two_in,
        target_in,
    )
    places = (feats, pos, spec, gain, probe, slot, count, w_rad, w_one, w_two, target)
    loads = [
        pltpu.make_async_copy(source, place, load_sem.at[i])
        for i, (source, place) in enumerate(zip(sources, places))
    ]
    for copy in loads:
        copy.start()
    for copy in loads:
        copy.wait()

    nspec = gain.shape[0]
    onehot = (lax.broadcasted_iota(jnp.int32, (nspec, natoms), 0) == spec[...]).astype(jnp.float32)
    gains = lax.dot_general(
        onehot,
        gain[...],
        (((0,), (0,)), ((), ())),
        precision=lax.Precision.HIGHEST,
        preferred_element_type=jnp.float32,
    )
    for (low, high), tab in zip(CHUNKS, tabs):
        for k in range(low, high):
            raw = feats[:, k * chans : (k + 1) * chans].astype(jnp.float32)
            tab[0, k - low] = (raw * gains).astype(jnp.bfloat16)
    posb[0] = pos[...]
    for block in range(nblocks):
        for axis in range(3):
            row = probe[axis : axis + 1, block * PBLK : (block + 1) * PBLK]
            pmap[block, axis] = jnp.transpose(jnp.broadcast_to(row, (PBLK, PBLK)))
    msg[...] = jnp.zeros_like(msg)
    pl.semaphore_wait(barrier, len(greeted) + 1)

    half = natoms // 2
    rows = pl.ds(pl.multiple_of(gz * half, half), half)

    def ici(c, xi, yi):
        tab = tabs[c]
        if yi == 0:
            source, dev = 0, at(-dxs[xi], 0)
        elif xi == 0:
            source, dev = 0, at(0, -dys[yi])
        elif c in Y_FIRST:
            source, dev = yi, at(-dxs[xi], 0)
        else:
            source, dev = xi * nyc, at(0, -dys[yi])
        col = xi * nyc + yi
        return pltpu.make_async_remote_copy(
            src_ref=tab.at[source, :, rows, :],
            dst_ref=tab.at[col, :, rows, :],
            send_sem=ici_send.at[c, col],
            recv_sem=ici_recv.at[c, col],
            device_id=dev,
            device_id_type=MESH,
        )

    def sib(c, xi, yi):
        tab = tabs[c]
        col = xi * nyc + yi
        return pltpu.make_async_remote_copy(
            src_ref=tab.at[col, :, rows, :],
            dst_ref=tab.at[col, :, rows, :],
            send_sem=sib_send.at[c, col],
            recv_sem=sib_recv.at[c, col],
            device_id=sibling,
            device_id_type=MESH,
        )

    def pos_copy(xi, yi):
        col = xi * nyc + yi
        return pltpu.make_async_remote_copy(
            src_ref=pos,
            dst_ref=posb.at[col],
            send_sem=pos_send.at[col],
            recv_sem=pos_recv.at[col],
            device_id=at(-dxs[xi], -dys[yi]),
            device_id_type=MESH,
        )

    along_x = [(xi, yi) for xi, yi in remote if yi == 0]
    along_y = [(xi, yi) for xi, yi in remote if xi == 0]
    second = [(xi, yi) for xi, yi in remote if xi != 0 and yi != 0]
    for xi, yi in remote:
        pos_copy(xi, yi).start()
    def start_y(c):
        for xi, yi in along_y:
            ici(c, xi, yi).start()

    for c in X_ORDER:
        for xi, yi in along_x:
            ici(c, xi, yi).start()
        if c == 0:
            start_y(0)
        elif c == 1:
            start_y(1)
            start_y(3)

    def pass_x(c):
        for xi, yi in along_x:
            ici(c, xi, yi).wait_recv()
            if c not in Y_FIRST:
                for sx, sy in second:
                    if sx == xi:
                        ici(c, sx, sy).start()
            sib(c, xi, yi).start()

    def pass_y(c):
        for xi, yi in along_y:
            ici(c, xi, yi).wait_recv()
            if c in Y_FIRST:
                for sx, sy in second:
                    if sy == yi:
                        ici(c, sx, sy).start()
            sib(c, xi, yi).start()

    def pass_second(c):
        for xi, yi in second:
            ici(c, xi, yi).wait_recv()
            sib(c, xi, yi).start()

    def column_of(block, entry):
        s = slot[block, entry]
        xi = lax.rem(s // 3 + 2, 3)
        yi = lax.rem(s % 3 + 1, 2) if ny == 2 else lax.rem(s % 3 + 2, 3)
        return xi * nyc + yi

    gamma = 0.5 * (nrad / cutoff) ** 2
    rc2 = cutoff * cutoff

    def edge_unit(unit, _):
        block = unit // nentry
        entry = unit % nentry
        s = slot[block, entry]
        shift_x = (s // 3 - 1).astype(jnp.float32)
        shift_y = (s % 3 - 1).astype(jnp.float32)
        used = (entry < count[block]).astype(jnp.float32)
        atoms = posb[column_of(block, entry)]
        ax = atoms[0] + shift_x
        ay = atoms[1] + shift_y
        az = atoms[2]

        def strip(i, _):
            at_row = pl.multiple_of(i * ROWS, ROWS)
            dist_x = (ax - pmap[block, 0, pl.ds(at_row, ROWS), :]) * side_x
            dist_y = (ay - pmap[block, 1, pl.ds(at_row, ROWS), :]) * side_y
            dist_z = (az - pmap[block, 2, pl.ds(at_row, ROWS), :]) * side_z
            radius2 = dist_x * dist_x + dist_y * dist_y + dist_z * dist_z
            smooth = jnp.where(radius2 < rc2, (1.0 - radius2 / rc2) ** 2, 0.0) * used
            radius = jnp.sqrt(radius2)
            hx, hy, hz = dist_x / cutoff, dist_y / cutoff, dist_z / cutoff
            harmonics = (
                None,
                hx,
                hy,
                hz,
                sqrt_three * hx * hy,
                sqrt_three * hy * hz,
                (3.0 * dist_z * dist_z - radius2) * (0.5 / rc2),
                sqrt_three * hx * hz,
                (0.5 * sqrt_three) * (hx * hx - hy * hy),
            )
            for b in range(nrad):
                offset = radius - cutoff * b / (nrad - 1)
                basis = jnp.exp(-gamma * (offset * offset)) * smooth
                for k in range(9):
                    value = basis if k == 0 else basis * harmonics[k]
                    edges[block, k, entry, pl.ds(b * PBLK + at_row, ROWS), :] = value.astype(
                        jnp.bfloat16
                    )
            return 0

        lax.fori_loop(0, PBLK // ROWS, strip, 0)
        return 0

    def matmul(*group):
        for c in group:
            for xi, yi in remote:
                sib(c, xi, yi).wait_recv()
        for block in range(nblocks):
            cols = [column_of(block, entry) for entry in range(nentry)]
            weights = jnp.concatenate(
                [
                    tabs[c][cols[entry], k - CHUNKS[c][0]]
                    for c in group
                    for k in range(*CHUNKS[c])
                    for entry in range(nentry)
                ],
                axis=0,
            )
            lhs = jnp.concatenate(
                [
                    edges[block, k, entry]
                    for c in group
                    for k in range(*CHUNKS[c])
                    for entry in range(nentry)
                ],
                axis=1,
            )
            part = jnp.dot(lhs, weights, preferred_element_type=jnp.float32)
            degree = DEGREE[group[0]]
            total = msg[block]
            for b in range(nrad):
                total = total + part[b * PBLK : (b + 1) * PBLK] * w_rad[degree, b : b + 1, :]
            msg[block] = total

    for xi, yi in remote:
        pos_copy(xi, yi).wait_recv()
    units = nblocks * nentry

    def edge_part(low, high):
        lax.fori_loop(low * units // 8, high * units // 8, edge_unit, 0)

    edge_part(0, 1)
    pass_y(0)
    pass_x(0)
    start_y(2)
    edge_part(1, 4)
    pass_y(1)
    pass_y(3)
    edge_part(4, 5)
    pass_x(1)
    start_y(4)
    edge_part(5, 8)
    pass_second(0)
    pass_y(2)
    pass_x(2)
    start_y(5)
    pass_x(4)
    pass_second(1)
    pass_x(5)
    matmul(0, 1)
    pass_y(4)
    pass_second(2)
    pass_x(3)
    pass_y(5)
    matmul(2)
    pass_second(4)
    pass_second(3)
    matmul(4)
    pass_second(5)
    matmul(3)
    matmul(5)

    message_bf = msg[...].reshape(nblocks * PBLK, chans).astype(jnp.bfloat16)
    pre = jnp.dot(message_bf, w_one[...], preferred_element_type=jnp.float32)
    sigm = jax.nn.sigmoid(pre)
    act = pre * sigm
    dens = jnp.sum(act * w_two[...], axis=1, keepdims=True)
    goals = []
    for block in range(nblocks):
        column = dens[block * PBLK : (block + 1) * PBLK]
        flat = jnp.transpose(jnp.broadcast_to(column, (PBLK, PBLK)))
        density_out[block : block + 1, :] = flat[0:1]
        goal = jnp.transpose(jnp.broadcast_to(target[block : block + 1, :], (PBLK, PBLK)))
        goals.append(goal[:, 0:1])
    goals = jnp.concatenate(goals, axis=0)
    total_probes = nblocks * PBLK * nx * ny * 2
    grad_out = (dens - goals) * jnp.float32(1.0 / math.sqrt(total_probes))
    dpre = (grad_out * w_two[...] * sigm * (1.0 + pre * (1.0 - sigm))).astype(jnp.bfloat16)
    local_one = lax.dot_general(
        message_bf, dpre, (((0,), (0,)), ((), ())), preferred_element_type=jnp.float32
    )
    local_two = jnp.sum(grad_out * act, axis=0, keepdims=True)
    if not reduce_refs:
        one_out[...] = local_one
        two_out[...] = local_two
    else:
        (
            part,
            two_part,
            pair_in,
            two_pair_in,
            shares,
            two_share,
            shares_in,
            two_in,
            gathered,
            two_total,
            pair_send,
            pair_recv,
            share_send,
            share_recv,
            two_send,
            two_recv,
            full_send,
            full_recv,
        ) = reduce_refs
        owners, span = gathered.shape[0], gathered.shape[1]
        first = (chips - owners) // 2
        mine = me - first
        owning = jnp.logical_and(mine >= 0, mine < owners)
        part[...] = local_one
        two_part[...] = local_two

        def to_sibling(index, source, dest):
            return pltpu.make_async_remote_copy(
                src_ref=source,
                dst_ref=dest,
                send_sem=pair_send.at[index],
                recv_sem=pair_recv.at[index],
                device_id=sibling,
                device_id_type=MESH,
            )

        def to_chip(chip, source, dest, send, recv):
            return pltpu.make_async_remote_copy(
                src_ref=source,
                dst_ref=dest,
                send_sem=send,
                recv_sem=recv,
                device_id={"gx": chip // ny, "gy": lax.rem(chip, ny)},
                device_id_type=MESH,
            )

        def share_copy(w, source_chip):
            return to_chip(
                first + w,
                shares.at[w],
                shares_in.at[source_chip],
                share_send.at[w],
                share_recv.at[source_chip],
            )

        def full_copy(chip, w):
            return to_chip(chip, gathered.at[w], gathered.at[w], full_send.at[chip], full_recv.at[w])

        def two_copy(chip, source_chip):
            return to_chip(
                chip, two_share, two_in.at[source_chip], two_send.at[chip], two_recv.at[source_chip]
            )

        def piece(w):
            return to_sibling(3 + w, gathered.at[w], gathered.at[w])

        swaps = [to_sibling(0, part, pair_in), to_sibling(1, two_part, two_pair_in)]
        two_back = to_sibling(2, two_total, two_total)
        others = [lax.rem(me + offset, chips) for offset in offsets]

        @pl.when(gz == 0)
        def _():
            for copy in swaps:
                copy.start()
            two_back.wait_recv()
            for w in range(owners):
                piece(w).wait_recv()
            for copy in swaps:
                copy.wait_send()

        @pl.when(gz == 1)
        def _():
            for copy in swaps:
                copy.wait_recv()
            chip_sum = part[...] + pair_in[...]
            shares[...] = chip_sum.reshape(owners, span, chans).astype(jnp.bfloat16)
            two_sum = two_part[...] + two_pair_in[...]
            two_share[...] = two_sum
            two_in[me] = two_sum
            for w in range(owners):

                @pl.when(mine != w)
                def _(w=w):
                    share_copy(w, me).start()

            for chip in others:
                two_copy(chip, me).start()

            @pl.when(owning)
            def _():
                total = shares[mine].astype(jnp.float32)
                for chip in others:
                    share_copy(mine, chip).wait_recv()
                    total = total + shares_in[chip].astype(jnp.float32)
                gathered[mine] = total.astype(jnp.bfloat16)
                for chip in others:
                    full_copy(chip, mine).start()
                piece(mine).start()

            for chip in others:
                two_copy(chip, chip).wait_recv()
            two_total[...] = jnp.sum(two_in[...], axis=0)
            two_back.start()
            for w in range(owners):

                @pl.when(mine != w)
                def _(w=w):
                    full_copy(me, w).wait_recv()
                    piece(w).start()

            for w in range(owners):

                @pl.when(mine != w)
                def _(w=w):
                    share_copy(w, me).wait_send()

                piece(w).wait_send()

            @pl.when(owning)
            def _():
                for chip in others:
                    full_copy(chip, mine).wait_send()

            for chip in others:
                two_copy(chip, me).wait_send()
            two_back.wait_send()

        one_out[...] = gathered[...].reshape(chans, chans)
        two_out[...] = two_total[...]

    for xi, yi in remote:
        pos_copy(xi, yi).wait_send()
        for c in range(len(CHUNKS)):
            ici(c, xi, yi).wait_send()
            sib(c, xi, yi).wait_send()


def on_device(
    nx,
    ny,
    atom_feats,
    atom_pos,
    species,
    species_gain,
    probe_pos,
    pair_slot,
    pair_count,
    w_rad,
    w_one,
    w_two,
    target,
):
    natoms = atom_feats.shape[2]
    chans = w_one.shape[0]
    nblocks = pair_slot.shape[0]
    nentry = pair_slot.shape[1]
    nrad = w_rad.shape[1]
    ncol = 6 if ny == 2 else 9
    vmem = pl.BlockSpec(memory_space=pltpu.VMEM)
    nchunk = len(CHUNKS)
    chips = nx * ny
    owners = (nx // 2 if nx % 4 == 0 else nx) * ny
    fused = chips <= FUSED_CHIPS and chans % (16 * owners) == 0
    reduce_scratch = []
    if fused:
        span = chans // owners
        reduce_scratch = [
            pltpu.VMEM((chans, chans), jnp.float32),
            pltpu.VMEM((1, chans), jnp.float32),
            pltpu.VMEM((chans, chans), jnp.float32),
            pltpu.VMEM((1, chans), jnp.float32),
            pltpu.VMEM((owners, span, chans), jnp.bfloat16),
            pltpu.VMEM((1, chans), jnp.float32),
            pltpu.VMEM((chips, span, chans), jnp.bfloat16),
            pltpu.VMEM((chips, 1, chans), jnp.float32),
            pltpu.VMEM((owners, span, chans), jnp.bfloat16),
            pltpu.VMEM((1, chans), jnp.float32),
            pltpu.SemaphoreType.DMA((3 + owners,)),
            pltpu.SemaphoreType.DMA((3 + owners,)),
            *[pltpu.SemaphoreType.DMA((chips,)) for _ in range(6)],
        ]
    operands = (
        atom_feats.reshape(natoms, -1),
        atom_pos.reshape(3, 1, natoms),
        species.reshape(1, natoms),
        species_gain,
        probe_pos,
        pair_slot,
        pair_count,
        w_rad,
        w_one,
        w_two.reshape(1, chans),
        target.reshape(nblocks, PBLK),
    )
    scalars = (5, 6)
    density, one, two = pl.pallas_call(
        functools.partial(kernel, nx, ny),
        out_shape=(
            jax.ShapeDtypeStruct((nblocks, PBLK), jnp.float32),
            jax.ShapeDtypeStruct((chans, chans), jnp.bfloat16 if fused else jnp.float32),
            jax.ShapeDtypeStruct((1, chans), jnp.float32),
        ),
        in_specs=[pl.BlockSpec(memory_space=pl.ANY)] * len(operands),
        out_specs=(vmem, vmem, vmem),
        scratch_shapes=[
            *[
                (pltpu.SMEM if i in scalars else pltpu.VMEM)(operand.shape, operand.dtype)
                for i, operand in enumerate(operands)
            ],
            pltpu.SemaphoreType.DMA((len(operands),)),
            *[
                pltpu.VMEM((ncol, high - low, natoms, chans), jnp.bfloat16)
                for low, high in CHUNKS
            ],
            pltpu.VMEM((ncol, 3, 1, natoms), jnp.float32),
            pltpu.VMEM((nblocks, 9, nentry, nrad * PBLK, natoms), jnp.bfloat16),
            pltpu.VMEM((nblocks, 3, PBLK, PBLK), jnp.float32),
            pltpu.VMEM((nblocks, PBLK, chans), jnp.float32),
            pltpu.SemaphoreType.DMA((nchunk, ncol)),
            pltpu.SemaphoreType.DMA((nchunk, ncol)),
            pltpu.SemaphoreType.DMA((nchunk, ncol)),
            pltpu.SemaphoreType.DMA((nchunk, ncol)),
            pltpu.SemaphoreType.DMA((ncol,)),
            pltpu.SemaphoreType.DMA((ncol,)),
            *reduce_scratch,
        ],
        compiler_params=pltpu.CompilerParams(
            collective_id=0, has_side_effects=True, vmem_limit_bytes=60 * 1024 * 1024
        ),
    )(*operands)
    two = two.reshape(chans)
    if fused:
        one = one.astype(jnp.float32)
    else:
        one, two = lax.psum((one, two), ("gx", "gy", "gz"))
    return density.reshape(-1), one, two


def solution(mesh):
    return jax.shard_map(
        functools.partial(on_device, mesh.shape["gx"], mesh.shape["gy"]),
        mesh=mesh,
        in_specs=(
            P(("grp", "gx"), "gy", None, None),
            P(("grp", "gx"), "gy", None, None),
            P(("grp", "gx"), "gy", None),
            P(),
            P(None, ("grp", "gx", "gy", "gz")),
            P(("grp", "gx", "gy", "gz"), None),
            P(("grp", "gx", "gy", "gz")),
            P(),
            P(),
            P(),
            P(("grp", "gx", "gy", "gz")),
        ),
        out_specs=(P(("grp", "gx", "gy", "gz")), P("grp", None), P("grp")),
        check_vma=False,
    )
```

```python
import functools
import math

import jax
import jax.numpy as jnp
from jax import lax
from jax.experimental import pallas as pl
from jax.experimental.pallas import tpu as pltpu
from jax.sharding import PartitionSpec as P

MESH = pl.DeviceIdType.MESH
PBLK = 128
side_x = 8.0
side_y = 8.0
side_z = 25.0
cutoff = 4.0
sqrt_three = 1.7320508075688772
CHUNKS = ((1, 2), (2, 4), (4, 6), (6, 8), (8, 9), (0, 1))
DEGREE = (1, 1, 2, 2, 2, 0)
Y_FIRST = (3,)
FUSED_CHIPS = 8
ROWS = 16


def kernel(
    nx,
    ny,
    feats_in,
    pos_in,
    spec_in,
    gain_in,
    probe_in,
    slot_in,
    count_in,
    w_rad_in,
    w_one_in,
    w_two_in,
    target_in,
    density_out,
    one_out,
    two_out,
    feats,
    pos,
    spec,
    gain,
    probe,
    slot,
    count,
    w_rad,
    w_one,
    w_two,
    target,
    load_sem,
    tab0,
    tab1,
    tab2,
    tab3,
    tab4,
    tab5,
    posb,
    edges,
    pmap,
    msg,
    ici_send,
    ici_recv,
    sib_send,
    sib_recv,
    pos_send,
    pos_recv,
    *reduce_refs,
):
    tabs = (tab0, tab1, tab2, tab3, tab4, tab5)
    nentry = slot.shape[1]
    nblocks = slot.shape[0]
    nrad = w_rad.shape[1]
    natoms, chans = tab0.shape[2], tab0.shape[3]
    dys = (0, 1) if ny == 2 else (0, 1, -1)
    dxs = (0, 1, -1)
    nyc = len(dys)
    ncol = 3 * nyc
    gx, gy, gz = lax.axis_index("gx"), lax.axis_index("gy"), lax.axis_index("gz")
    sibling = {"gz": 1 - gz}

    def at(dx, dy):
        return {"gx": lax.rem(gx + dx + nx, nx), "gy": lax.rem(gy + dy + ny, ny)}

    remote = [(xi, yi) for xi in range(3) for yi in range(nyc) if (xi, yi) != (0, 0)]
    chips = nx * ny
    me = gx * ny + gy
    offsets = range(1, chips)

    def peer(offset):
        other = lax.rem(me + offset, chips)
        return {"gx": other // ny, "gy": lax.rem(other, ny)}

    barrier = pltpu.get_barrier_semaphore()
    if reduce_refs:
        greeted = [peer(offset) for offset in offsets]
    else:
        greeted = [at(-dxs[xi], -dys[yi]) for xi, yi in remote]
    for device in greeted:
        pl.semaphore_signal(barrier, inc=1, device_id=device, device_id_type=MESH)
    pl.semaphore_signal(barrier, inc=1, device_id=sibling, device_id_type=MESH)
    sources = (
        feats_in,
        pos_in,
        spec_in,
        gain_in,
        probe_in,
        slot_in,
        count_in,
        w_rad_in,
        w_one_in,
        w_two_in,
        target_in,
    )
    places = (feats, pos, spec, gain, probe, slot, count, w_rad, w_one, w_two, target)
    loads = [
        pltpu.make_async_copy(source, place, load_sem.at[i])
        for i, (source, place) in enumerate(zip(sources, places))
    ]
    for copy in loads:
        copy.start()
    for copy in loads:
        copy.wait()

    nspec = gain.shape[0]
    onehot = (lax.broadcasted_iota(jnp.int32, (nspec, natoms), 0) == spec[...]).astype(jnp.float32)
    gains = lax.dot_general(
        onehot,
        gain[...],
        (((0,), (0,)), ((), ())),
        precision=lax.Precision.HIGHEST,
        preferred_element_type=jnp.float32,
    )
    for (low, high), tab in zip(CHUNKS, tabs):
        for k in range(low, high):
            raw = feats[:, k * chans : (k + 1) * chans].astype(jnp.float32)
            tab[0, k - low] = (raw * gains).astype(jnp.bfloat16)
    posb[0] = pos[...]
    for block in range(nblocks):
        for axis in range(3):
            row = probe[axis : axis + 1, block * PBLK : (block + 1) * PBLK]
            pmap[block, axis] = jnp.transpose(jnp.broadcast_to(row, (PBLK, PBLK)))
    msg[...] = jnp.zeros_like(msg)
    pl.semaphore_wait(barrier, len(greeted) + 1)

    half = natoms // 2
    rows = pl.ds(pl.multiple_of(gz * half, half), half)

    def ici(c, xi, yi):
        tab = tabs[c]
        if yi == 0:
            source, dev = 0, at(-dxs[xi], 0)
        elif xi == 0:
            source, dev = 0, at(0, -dys[yi])
        elif c in Y_FIRST:
            source, dev = yi, at(-dxs[xi], 0)
        else:
            source, dev = xi * nyc, at(0, -dys[yi])
        col = xi * nyc + yi
        return pltpu.make_async_remote_copy(
            src_ref=tab.at[source, :, rows, :],
            dst_ref=tab.at[col, :, rows, :],
            send_sem=ici_send.at[c, col],
            recv_sem=ici_recv.at[c, col],
            device_id=dev,
            device_id_type=MESH,
        )

    def sib(c, xi, yi):
        tab = tabs[c]
        col = xi * nyc + yi
        return pltpu.make_async_remote_copy(
            src_ref=tab.at[col, :, rows, :],
            dst_ref=tab.at[col, :, rows, :],
            send_sem=sib_send.at[c, col],
            recv_sem=sib_recv.at[c, col],
            device_id=sibling,
            device_id_type=MESH,
        )

    def pos_copy(xi, yi):
        col = xi * nyc + yi
        return pltpu.make_async_remote_copy(
            src_ref=pos,
            dst_ref=posb.at[col],
            send_sem=pos_send.at[col],
            recv_sem=pos_recv.at[col],
            device_id=at(-dxs[xi], -dys[yi]),
            device_id_type=MESH,
        )

    along_x = [(xi, yi) for xi, yi in remote if yi == 0]
    along_y = [(xi, yi) for xi, yi in remote if xi == 0]
    second = [(xi, yi) for xi, yi in remote if xi != 0 and yi != 0]
    for xi, yi in remote:
        pos_copy(xi, yi).start()
    def start_y(c):
        for xi, yi in along_y:
            ici(c, xi, yi).start()

    def start_x(c):
        for xi, yi in along_x:
            ici(c, xi, yi).start()

    start_y(3)
    for c in (0, 1, 2, 4, 5):
        start_x(c)
        start_y(c)
    start_x(3)

    def pass_x(c):
        for xi, yi in along_x:
            ici(c, xi, yi).wait_recv()
            if c not in Y_FIRST:
                for sx, sy in second:
                    if sx == xi:
                        ici(c, sx, sy).start()
            sib(c, xi, yi).start()

    def pass_y(c):
        for xi, yi in along_y:
            ici(c, xi, yi).wait_recv()
            if c in Y_FIRST:
                for sx, sy in second:
                    if sy == yi:
                        ici(c, sx, sy).start()
            sib(c, xi, yi).start()

    def pass_second(c):
        for xi, yi in second:
            ici(c, xi, yi).wait_recv()
            sib(c, xi, yi).start()

    def column_of(block, entry):
        s = slot[block, entry]
        xi = lax.rem(s // 3 + 2, 3)
        yi = lax.rem(s % 3 + 1, 2) if ny == 2 else lax.rem(s % 3 + 2, 3)
        return xi * nyc + yi

    gamma = 0.5 * (nrad / cutoff) ** 2
    rc2 = cutoff * cutoff

    def edge_unit(unit, _):
        block = unit // nentry
        entry = unit % nentry
        s = slot[block, entry]
        shift_x = (s // 3 - 1).astype(jnp.float32)
        shift_y = (s % 3 - 1).astype(jnp.float32)
        used = (entry < count[block]).astype(jnp.float32)
        atoms = posb[column_of(block, entry)]
        ax = atoms[0] + shift_x
        ay = atoms[1] + shift_y
        az = atoms[2]

        def strip(i, _):
            at_row = pl.multiple_of(i * ROWS, ROWS)
            dist_x = (ax - pmap[block, 0, pl.ds(at_row, ROWS), :]) * side_x
            dist_y = (ay - pmap[block, 1, pl.ds(at_row, ROWS), :]) * side_y
            dist_z = (az - pmap[block, 2, pl.ds(at_row, ROWS), :]) * side_z
            radius2 = dist_x * dist_x + dist_y * dist_y + dist_z * dist_z
            smooth = jnp.where(radius2 < rc2, (1.0 - radius2 / rc2) ** 2, 0.0) * used
            radius = jnp.sqrt(radius2)
            hx, hy, hz = dist_x / cutoff, dist_y / cutoff, dist_z / cutoff
            harmonics = (
                None,
                hx,
                hy,
                hz,
                sqrt_three * hx * hy,
                sqrt_three * hy * hz,
                (3.0 * dist_z * dist_z - radius2) * (0.5 / rc2),
                sqrt_three * hx * hz,
                (0.5 * sqrt_three) * (hx * hx - hy * hy),
            )
            for b in range(nrad):
                offset = radius - cutoff * b / (nrad - 1)
                basis = jnp.exp(-gamma * (offset * offset)) * smooth
                for k in range(9):
                    value = basis if k == 0 else basis * harmonics[k]
                    edges[block, k, entry, pl.ds(b * PBLK + at_row, ROWS), :] = value.astype(
                        jnp.bfloat16
                    )
            return 0

        lax.fori_loop(0, PBLK // ROWS, strip, 0)
        return 0

    def matmul(*group):
        for c in group:
            for xi, yi in remote:
                sib(c, xi, yi).wait_recv()
        for block in range(nblocks):
            cols = [column_of(block, entry) for entry in range(nentry)]
            weights = jnp.concatenate(
                [
                    tabs[c][cols[entry], k - CHUNKS[c][0]]
                    for c in group
                    for k in range(*CHUNKS[c])
                    for entry in range(nentry)
                ],
                axis=0,
            )
            lhs = jnp.concatenate(
                [
                    edges[block, k, entry]
                    for c in group
                    for k in range(*CHUNKS[c])
                    for entry in range(nentry)
                ],
                axis=1,
            )
            part = jnp.dot(lhs, weights, preferred_element_type=jnp.float32)
            degree = DEGREE[group[0]]
            total = msg[block]
            for b in range(nrad):
                total = total + part[b * PBLK : (b + 1) * PBLK] * w_rad[degree, b : b + 1, :]
            msg[block] = total

    for xi, yi in remote:
        pos_copy(xi, yi).wait_recv()
    units = nblocks * nentry

    def edge_part(low, high):
        lax.fori_loop(low * units // 8, high * units // 8, edge_unit, 0)

    edge_part(0, 1)
    pass_y(3)
    pass_y(0)
    pass_x(0)
    edge_part(1, 5)
    pass_y(1)
    pass_x(1)
    edge_part(5, 8)
    pass_y(2)
    pass_x(2)
    pass_second(0)
    pass_x(4)
    pass_second(1)
    pass_x(5)
    matmul(0, 1)
    pass_y(4)
    pass_y(5)
    pass_second(2)
    pass_x(3)
    matmul(2)
    pass_second(4)
    pass_second(3)
    matmul(4)
    pass_second(5)
    matmul(3)
    matmul(5)

    message_bf = msg[...].reshape(nblocks * PBLK, chans).astype(jnp.bfloat16)
    pre = jnp.dot(message_bf, w_one[...], preferred_element_type=jnp.float32)
    sigm = jax.nn.sigmoid(pre)
    act = pre * sigm
    dens = jnp.sum(act * w_two[...], axis=1, keepdims=True)
    goals = []
    for block in range(nblocks):
        column = dens[block * PBLK : (block + 1) * PBLK]
        flat = jnp.transpose(jnp.broadcast_to(column, (PBLK, PBLK)))
        density_out[block : block + 1, :] = flat[0:1]
        goal = jnp.transpose(jnp.broadcast_to(target[block : block + 1, :], (PBLK, PBLK)))
        goals.append(goal[:, 0:1])
    goals = jnp.concatenate(goals, axis=0)
    total_probes = nblocks * PBLK * nx * ny * 2
    grad_out = (dens - goals) * jnp.float32(1.0 / math.sqrt(total_probes))
    dpre = (grad_out * w_two[...] * sigm * (1.0 + pre * (1.0 - sigm))).astype(jnp.bfloat16)
    local_one = lax.dot_general(
        message_bf, dpre, (((0,), (0,)), ((), ())), preferred_element_type=jnp.float32
    )
    local_two = jnp.sum(grad_out * act, axis=0, keepdims=True)
    if not reduce_refs:
        one_out[...] = local_one
        two_out[...] = local_two
    else:
        (
            part,
            two_part,
            pair_in,
            two_pair_in,
            shares,
            two_share,
            shares_in,
            two_in,
            gathered,
            two_total,
            pair_send,
            pair_recv,
            share_send,
            share_recv,
            two_send,
            two_recv,
            full_send,
            full_recv,
        ) = reduce_refs
        owners, span = gathered.shape[0], gathered.shape[1]
        first = (chips - owners) // 2
        mine = me - first
        owning = jnp.logical_and(mine >= 0, mine < owners)
        part[...] = local_one
        two_part[...] = local_two

        def to_sibling(index, source, dest):
            return pltpu.make_async_remote_copy(
                src_ref=source,
                dst_ref=dest,
                send_sem=pair_send.at[index],
                recv_sem=pair_recv.at[index],
                device_id=sibling,
                device_id_type=MESH,
            )

        def to_chip(chip, source, dest, send, recv):
            return pltpu.make_async_remote_copy(
                src_ref=source,
                dst_ref=dest,
                send_sem=send,
                recv_sem=recv,
                device_id={"gx": chip // ny, "gy": lax.rem(chip, ny)},
                device_id_type=MESH,
            )

        def share_copy(w, source_chip):
            return to_chip(
                first + w,
                shares.at[w],
                shares_in.at[source_chip],
                share_send.at[w],
                share_recv.at[source_chip],
            )

        def full_copy(chip, w):
            return to_chip(chip, gathered.at[w], gathered.at[w], full_send.at[chip], full_recv.at[w])

        def two_copy(chip, source_chip):
            return to_chip(
                chip, two_share, two_in.at[source_chip], two_send.at[chip], two_recv.at[source_chip]
            )

        def piece(w):
            return to_sibling(3 + w, gathered.at[w], gathered.at[w])

        swaps = [to_sibling(0, part, pair_in), to_sibling(1, two_part, two_pair_in)]
        two_back = to_sibling(2, two_total, two_total)
        others = [lax.rem(me + offset, chips) for offset in offsets]

        @pl.when(gz == 0)
        def _():
            for copy in swaps:
                copy.start()
            two_back.wait_recv()
            for w in range(owners):
                piece(w).wait_recv()
            for copy in swaps:
                copy.wait_send()

        @pl.when(gz == 1)
        def _():
            for copy in swaps:
                copy.wait_recv()
            chip_sum = part[...] + pair_in[...]
            shares[...] = chip_sum.reshape(owners, span, chans).astype(jnp.bfloat16)
            two_sum = two_part[...] + two_pair_in[...]
            two_share[...] = two_sum
            two_in[me] = two_sum
            for w in range(owners):

                @pl.when(mine != w)
                def _(w=w):
                    share_copy(w, me).start()

            for chip in others:
                two_copy(chip, me).start()

            @pl.when(owning)
            def _():
                total = shares[mine].astype(jnp.float32)
                for chip in others:
                    share_copy(mine, chip).wait_recv()
                    total = total + shares_in[chip].astype(jnp.float32)
                gathered[mine] = total.astype(jnp.bfloat16)
                for chip in others:
                    full_copy(chip, mine).start()
                piece(mine).start()

            for chip in others:
                two_copy(chip, chip).wait_recv()
            two_total[...] = jnp.sum(two_in[...], axis=0)
            two_back.start()
            for w in range(owners):

                @pl.when(mine != w)
                def _(w=w):
                    full_copy(me, w).wait_recv()
                    piece(w).start()

            for w in range(owners):

                @pl.when(mine != w)
                def _(w=w):
                    share_copy(w, me).wait_send()

                piece(w).wait_send()

            @pl.when(owning)
            def _():
                for chip in others:
                    full_copy(chip, mine).wait_send()

            for chip in others:
                two_copy(chip, me).wait_send()
            two_back.wait_send()

        one_out[...] = gathered[...].reshape(chans, chans)
        two_out[...] = two_total[...]

    for xi, yi in remote:
        pos_copy(xi, yi).wait_send()
        for c in range(len(CHUNKS)):
            ici(c, xi, yi).wait_send()
            sib(c, xi, yi).wait_send()


def on_device(
    nx,
    ny,
    atom_feats,
    atom_pos,
    species,
    species_gain,
    probe_pos,
    pair_slot,
    pair_count,
    w_rad,
    w_one,
    w_two,
    target,
):
    natoms = atom_feats.shape[2]
    chans = w_one.shape[0]
    nblocks = pair_slot.shape[0]
    nentry = pair_slot.shape[1]
    nrad = w_rad.shape[1]
    ncol = 6 if ny == 2 else 9
    vmem = pl.BlockSpec(memory_space=pltpu.VMEM)
    nchunk = len(CHUNKS)
    chips = nx * ny
    owners = (nx // 2 if nx % 4 == 0 else nx) * ny
    fused = chips <= FUSED_CHIPS and chans % (16 * owners) == 0
    reduce_scratch = []
    if fused:
        span = chans // owners
        reduce_scratch = [
            pltpu.VMEM((chans, chans), jnp.float32),
            pltpu.VMEM((1, chans), jnp.float32),
            pltpu.VMEM((chans, chans), jnp.float32),
            pltpu.VMEM((1, chans), jnp.float32),
            pltpu.VMEM((owners, span, chans), jnp.bfloat16),
            pltpu.VMEM((1, chans), jnp.float32),
            pltpu.VMEM((chips, span, chans), jnp.bfloat16),
            pltpu.VMEM((chips, 1, chans), jnp.float32),
            pltpu.VMEM((owners, span, chans), jnp.bfloat16),
            pltpu.VMEM((1, chans), jnp.float32),
            pltpu.SemaphoreType.DMA((3 + owners,)),
            pltpu.SemaphoreType.DMA((3 + owners,)),
            *[pltpu.SemaphoreType.DMA((chips,)) for _ in range(6)],
        ]
    operands = (
        atom_feats.reshape(natoms, -1),
        atom_pos.reshape(3, 1, natoms),
        species.reshape(1, natoms),
        species_gain,
        probe_pos,
        pair_slot,
        pair_count,
        w_rad,
        w_one,
        w_two.reshape(1, chans),
        target.reshape(nblocks, PBLK),
    )
    scalars = (5, 6)
    density, one, two = pl.pallas_call(
        functools.partial(kernel, nx, ny),
        out_shape=(
            pltpu.VMEM((nblocks, PBLK), jnp.float32),
            pltpu.VMEM((chans, chans), jnp.bfloat16 if fused else jnp.float32),
            pltpu.VMEM((1, chans), jnp.float32),
        ),
        in_specs=[pl.BlockSpec(memory_space=pl.ANY)] * len(operands),
        out_specs=(vmem, vmem, vmem),
        scratch_shapes=[
            *[
                (pltpu.SMEM if i in scalars else pltpu.VMEM)(operand.shape, operand.dtype)
                for i, operand in enumerate(operands)
            ],
            pltpu.SemaphoreType.DMA((len(operands),)),
            *[
                pltpu.VMEM((ncol, high - low, natoms, chans), jnp.bfloat16)
                for low, high in CHUNKS
            ],
            pltpu.VMEM((ncol, 3, 1, natoms), jnp.float32),
            pltpu.VMEM((nblocks, 9, nentry, nrad * PBLK, natoms), jnp.bfloat16),
            pltpu.VMEM((nblocks, 3, PBLK, PBLK), jnp.float32),
            pltpu.VMEM((nblocks, PBLK, chans), jnp.float32),
            pltpu.SemaphoreType.DMA((nchunk, ncol)),
            pltpu.SemaphoreType.DMA((nchunk, ncol)),
            pltpu.SemaphoreType.DMA((nchunk, ncol)),
            pltpu.SemaphoreType.DMA((nchunk, ncol)),
            pltpu.SemaphoreType.DMA((ncol,)),
            pltpu.SemaphoreType.DMA((ncol,)),
            *reduce_scratch,
        ],
        compiler_params=pltpu.CompilerParams(
            collective_id=0, has_side_effects=True, vmem_limit_bytes=60 * 1024 * 1024
        ),
    )(*operands)
    two = two.reshape(chans)
    if fused:
        one = one.astype(jnp.float32)
    else:
        one, two = lax.psum((one, two), ("gx", "gy", "gz"))
    return density.reshape(-1), one, two


def solution(mesh):
    return jax.shard_map(
        functools.partial(on_device, mesh.shape["gx"], mesh.shape["gy"]),
        mesh=mesh,
        in_specs=(
            P(("grp", "gx"), "gy", None, None),
            P(("grp", "gx"), "gy", None, None),
            P(("grp", "gx"), "gy", None),
            P(),
            P(None, ("grp", "gx", "gy", "gz")),
            P(("grp", "gx", "gy", "gz"), None),
            P(("grp", "gx", "gy", "gz")),
            P(),
            P(),
            P(),
            P(("grp", "gx", "gy", "gz")),
        ),
        out_specs=(P(("grp", "gx", "gy", "gz")), P("grp", None), P("grp")),
        check_vma=False,
    )
```
